32 devices in a mesh: grp: 2 (over y), tm: 4 (over z), row: 4 (over x, core).
Axes of the slice: x: 2, y: 2, z: 4, core: 2. Of those that a mesh axis runs over, the one named last changes fastest.
Arguments:
- frames: bfloat16 [16, 8, 24, 512], P(('grp', 'tm'), 'row'), parts along dimension 0, may hold values from -6 to 6
- w_in: bfloat16 [3, 3, 512, 512], P(None, None, None, ('tm', 'row')), may hold values from -0.046875 to 0.046875
- w_out: bfloat16 [3, 3, 512, 512], P(None, None, None, ('tm', 'row')), may hold values from -0.09375 to 0.09375
- decay_codes: int32 [512], replicated, may hold values from 0 to 15
- resets: int32 [16], P(('grp', 'tm')), parts along dimension 0, may hold values from 0 to 1, as said below
Outputs:
- mixed: bfloat16 [16, 8, 24, 512], P(('grp', 'tm'), 'row'), parts along dimension 0
The draws below stay inside these ranges and needn't reach their ends.
There are 2 independent parts, one for each index of `grp`. The reference program is written for one: setup_inputs(seed, part) draws one part's arguments, and reference() takes and returns one part's arrays. A program takes and returns all parts, laid end to end along the dimension named above; an argument that names none is the same for every part. Nothing has to cross between parts.
Inputs may be any that keep to these rules, and one draw needn't show every extreme that they name: `decay_codes`: an entry of the table of 16 decays. `resets`: some frames start an episode and some do not.
All inputs are finite; a program needn't handle non-finite values.
Results may differ from the reference program's by a relative error of at most 0.005.
Values may be sent and summed in bfloat16 or wider, within the bound.
No kernel may reach another device: no remote copies, remote signals or barrier semaphores. Data moves between devices by JAX's collectives and lax.ppermute only.
A program may use at most 64 MiB of HBM per device.

```python
import math
import jax
import jax.numpy as jnp
from jax import lax

C = 512
COLS = 24
LEVELS = 16
WINDOW = 4096
FRAMES = 8
HEIGHT = 8


def draw_resets(key, part):
    key_base, key_one, key_zero = jax.random.split(key, 3)
    rolled = jax.random.randint(key_base, (FRAMES,), 0, 6)
    base = (rolled == 0).astype(jnp.int32)
    first_pos = jax.random.randint(key_one, (), 0, FRAMES)
    offset = jax.random.randint(key_zero, (), 1, FRAMES)
    second_pos = (first_pos + offset) % FRAMES
    positions = jnp.arange(FRAMES, dtype=jnp.int32)
    with_one = jnp.where(positions == first_pos, 1, base)
    return jnp.where(positions == second_pos, 0, with_one).astype(jnp.int32)


def place_ends(array, rng, smallest, top_value):
    place = [jax.random.randint(jax.random.fold_in(rng, axis), (), 0, length) for axis, length in enumerate(array.shape)]
    longest = array.shape.index(max(array.shape))
    beside = place[:longest] + [(place[longest] + 1) % array.shape[longest]] + place[longest + 1:]
    return array.at[tuple(place)].set(smallest).at[tuple(beside)].set(top_value)


def block_scale(key, extent, cuts, low, top_value):
    gain, own = 1.0, jax.random.fold_in(key, 6)
    for position, shards_of in cuts:
        heights = jnp.exp(jax.random.uniform(jax.random.fold_in(own, position), (shards_of,), jnp.float32, low / len(cuts), top_value / len(cuts)))
        gain = gain * jnp.repeat(heights, extent[position] // shards_of).reshape([-1 if axis == position else 1 for axis in range(len(extent))])
    return gain


def noise(key, dims, deviation, reach, cuts=(), kind=jnp.bfloat16):
    factor_of = block_scale(key, dims, cuts, -0.22, 0.18) if cuts else 1.0
    values = jax.random.normal(key, dims, jnp.float32) * deviation * factor_of
    return jnp.minimum(jnp.maximum(values, -reach), reach).astype(kind)


def setup_inputs(seed: int = 0, part: int = 0) -> dict:
    arg_keys = jax.random.split(jax.random.key(seed), 6)
    part_splits = jax.random.split(jax.random.fold_in(arg_keys[5], part), 6)
    frames = noise(part_splits[0], (FRAMES, HEIGHT, COLS, C), 1.0, 6.0, ((0, 4), (1, 4)))
    w_in = noise(arg_keys[1], (3, 3, C, C), (36 * C) ** -0.5, 0.046875, ((3, 16),))
    w_out = noise(arg_keys[2], (3, 3, C, C), (9 * C) ** -0.5, 0.09375, ((3, 16),))
    decay_codes = place_ends(jax.random.randint(arg_keys[3], (C,), 0, LEVELS), jax.random.fold_in(arg_keys[3], 1), 0, LEVELS - 1).astype(jnp.int32)
    resets = draw_resets(jax.random.fold_in(jax.random.fold_in(arg_keys[5], part), 71), part)
    return dict(frames=frames, w_in=w_in, w_out=w_out, decay_codes=decay_codes, resets=resets)


LOW_LOG = math.log(0.995)
HIGH_LOG = math.log(0.9999)


def frame_rates(decay_codes, frame_count):
    levels = jnp.arange(LEVELS, dtype=jnp.int32)
    log_table = LOW_LOG + (levels.astype(jnp.float32) / (LEVELS - 1)) * (HIGH_LOG - LOW_LOG)
    picked = (decay_codes[:, None] == levels[None, :]).astype(jnp.float32)
    log_rate = jnp.sum(picked * log_table[None, :], axis=1)
    return jnp.exp((WINDOW / frame_count) * log_rate)


def conv_frame(image, weight):
    height, width = image.shape[0], image.shape[1]
    padded = jnp.pad(image, ((1, 1), (1, 1), (0, 0)))
    total = jnp.zeros((height * width, weight.shape[3]), jnp.float32)
    for i in range(3):
        for j in range(3):
            window = padded[i:i + height, j:j + width].reshape(height * width, -1)
            total = total + jnp.dot(window, weight[i, j], preferred_element_type=jnp.float32)
    return total.reshape(height, width, -1)


def reference(frames, w_in, w_out, decay_codes, resets):
    rates = frame_rates(decay_codes, FRAMES)
    gates = (1.0 - resets.astype(jnp.float32))[:, None] * rates[None, :]

    def advance(state, inputs):
        frame, gate = inputs
        drive = conv_frame(frame, w_in)
        state = gate[None, None, :] * state + drive
        hidden = jax.nn.gelu(state).astype(jnp.bfloat16)
        return state, conv_frame(hidden, w_out).astype(jnp.bfloat16)

    initial = jnp.zeros((HEIGHT, COLS, C), jnp.float32)
    _, mixed = lax.scan(advance, initial, (frames, gates))
    return mixed
```

```python
import functools
import math

import jax
import jax.numpy as jnp
from jax import lax
from jax.experimental import pallas as pl
from jax.experimental.pallas import tpu as pltpu
from jax.sharding import PartitionSpec as P

LEVELS = 16
WINDOW = 4096


LOW_LOG = math.log(0.995)
HIGH_LOG = math.log(0.9999)


def entering(part, axis, combine, identity):
    place = lax.axis_index(axis)
    gathered = jax.tree.map(lambda a: lax.all_gather(a, axis), part)
    state = jax.tree.map(lambda a, e: jnp.zeros_like(a) + jnp.asarray(e, a.dtype), part, identity)

    def one(turn, state):
        return combine(
            state, jax.tree.map(lambda a: lax.dynamic_index_in_dim(a, turn, 0, False), gathered)
        )

    return lax.fori_loop(0, place, one, state)


def extended_2(array, sides, width):
    for axis, dim in sides:
        size, length = (lax.axis_size(axis), array.shape[dim])
        up = [(i, (i + 1) % size) for i in range(size - 1)]
        down = [(j, i) for i, j in up]
        last = lax.slice_in_dim(array, length - width, length, axis=dim)
        initial = lax.slice_in_dim(array, 0, width, axis=dim)
        before = lax.ppermute(last, axis, up)
        after = lax.ppermute(initial, axis, down)
        array = jnp.concatenate([before, array, after], axis=dim)
    return array


def frame_rates(decay_codes, frame_count):
    levels = jnp.arange(LEVELS, dtype=jnp.int32)
    log_table = LOW_LOG + levels.astype(jnp.float32) / (LEVELS - 1) * (HIGH_LOG - LOW_LOG)
    picked = (decay_codes[:, None] == levels[None, :]).astype(jnp.float32)
    log_rate = jnp.sum(picked * log_table[None, :], axis=1)
    return jnp.exp(WINDOW / frame_count * log_rate)


def conv_rows(rows, weight):
    count, height, width = (rows.shape[0], rows.shape[1] - 2, rows.shape[2])
    padded = jnp.pad(rows, ((0, 0), (0, 0), (1, 1), (0, 0)))
    total = jnp.zeros((count, height, width, weight.shape[3]), jnp.float32)
    for i in range(3):
        for j in range(3):
            total = total + jnp.einsum(
                "frwc,ck->frwk",
                padded[:, i : i + height, j : j + width],
                weight[i, j],
                preferred_element_type=jnp.float32,
            )
    return total


def carry_combine(earlier, later):
    return (earlier[0] * later[0], later[0][None, None, :] * earlier[1] + later[1])


def recurrence(drive, gates):

    def advance(carry, inputs):
        state, product = carry
        frame_drive, gate = inputs
        state = gate[None, None, :] * state + frame_drive
        product = product * gate
        return ((state, product), (state, product))

    start = (jnp.zeros(drive.shape[1:], jnp.float32), jnp.ones((drive.shape[3],), jnp.float32))
    (last_state, last_product), (states, products) = lax.scan(advance, start, (drive, gates))
    identity = (jnp.ones_like(last_product), jnp.zeros_like(last_state))
    before_product, before_state = entering(
        (last_product, last_state), "tm", carry_combine, identity
    )
    return states + products[:, None, None, :] * before_state[None]


def on_device(frames, w_in, w_out, decay_codes, resets):
    frame_count = frames.shape[0] * lax.axis_size("tm")
    rates = frame_rates(decay_codes, frame_count)
    gates = (1.0 - resets.astype(jnp.float32))[:, None] * rates[None, :]
    extended = extended_2(frames, (("row", 1),), 1)
    state = recurrence(
        conv_rows(extended, lax.all_gather(w_in, ("tm", "row"), axis=3, tiled=True)), gates
    )
    hidden = jax.nn.gelu(state).astype(jnp.bfloat16)
    hidden_rows = extended_2(hidden, (("row", 1),), 1)
    return conv_rows(hidden_rows, lax.all_gather(w_out, ("tm", "row"), axis=3, tiled=True)).astype(
        jnp.bfloat16
    )


BF16 = jnp.bfloat16
F32 = jnp.float32
VMEM = pl.BlockSpec(memory_space=pltpu.VMEM)


def swapped(array, axis, distance):
    size = lax.axis_size(axis)
    return lax.ppermute(array, axis, [(i, i ^ distance) for i in range(size)])


def dot_nt(a, b):
    return lax.dot_general(a, b, (((1,), (1,)), ((), ())), preferred_element_type=F32)


def shifted_columns(flat, offset, width):
    if offset == 0:
        return flat
    length = flat.shape[0]
    column = lax.rem(lax.broadcasted_iota(jnp.int32, flat.shape, 0), width)
    edge = 0 if offset < 0 else width - 1
    return jnp.where(column == edge, 0.0, pltpu.roll(flat, (-offset) % length, 0))


def drive_kernel(
    dims, f0, f1, f2, f3, up, down, w0, w1, w2, w3, codes, hid, x, w, gates, states
):
    count, height, width, frame_total = dims
    blocks = count * width
    z, r = lax.axis_index("tm"), lax.axis_index("row")
    rate = WINDOW / frame_total
    code = codes[pl.ds(z, 1), :].astype(F32)
    rates = jnp.exp(rate * (LOW_LOG + code / (LEVELS - 1) * (HIGH_LOG - LOW_LOG)))
    lanes = rates.shape[1]
    for d, f in enumerate((f0, f1, f2, f3)):
        at = z ^ d
        here = pl.ds(pl.multiple_of(at * blocks, blocks), blocks)
        x[0, here, :] = up[d]
        for row in range(height):
            x[1 + row, here, :] = f[row * blocks : (row + 1) * blocks, :]
        x[1 + height, here, :] = down[d]
        marks = f[height * blocks :, :lanes].astype(F32)
        for k in range(count):
            gates[pl.ds(at * count + k, 1), :] = (1.0 - marks[k : k + 1, :]) * rates
    for d, block in enumerate((w0, w1, w2, w3)):
        for i in range(3):
            for j in range(3):
                w[i, j, pl.ds(r ^ d, 1)] = block[i, j][None]
    slab = x.shape[1]
    total = None
    for i in range(3):
        rows = x[i : i + height].reshape(height * slab, x.shape[2])
        term = dot_nt(rows, w[i].reshape(3 * lanes, x.shape[2]))
        total = term if total is None else total + term
    drive = total[:, lanes : 2 * lanes]
    drive = drive + shifted_columns(total[:, :lanes], -1, width)
    drive = drive + shifted_columns(total[:, 2 * lanes :], 1, width)
    for row in range(height):
        state = jnp.zeros((width, lanes), F32)
        for t in range(frame_total):
            first = row * slab + t * width
            state = gates[t : t + 1, :] * state + drive[first : first + width]
            states[first : first + width, :] = state
    for row in range(height):
        hid[row] = jax.nn.gelu(states[row * slab : (row + 1) * slab, :]).astype(BF16)


def mix_kernel(dims, hid, up, down, w0, w1, w2, w3, p0, p1, p2, p3, a, w, part):
    count, height, width = dims
    z, r = lax.axis_index("tm"), lax.axis_index("row")
    outs, lanes = w0.shape[3], w0.shape[4]
    for d, block in enumerate((w0, w1, w2, w3)):
        for e in range(4):
            slot = (z ^ e) * 4 + (r ^ d)
            here = pl.ds(pl.multiple_of(slot * outs, outs), outs)
            for i in range(3):
                for j in range(3):
                    tap = 3 * i + j
                    w[here, tap * lanes : (tap + 1) * lanes] = block[e, i, j]
    slab = hid.shape[1]
    for row in range(height + 2):
        ref = up if row == 0 else down if row == height + 1 else hid
        values = ref[0 if row in (0, height + 1) else row - 1].astype(F32)
        for j in range(3):
            moved = shifted_columns(values, j - 1, width).astype(BF16)
            for i in range(3):
                out_row = row - i
                if 0 <= out_row < height:
                    tap = 3 * i + j
                    a[out_row, :, tap * lanes : (tap + 1) * lanes] = moved
    for row in range(height):
        part[row] = dot_nt(a[row], w[...])
    blocks = count * width
    for d, out in enumerate((p0, p1, p2, p3)):
        here = pl.ds(pl.multiple_of((z ^ d) * blocks, blocks), blocks)
        for row in range(height):
            out[row] = part[row, here, :].astype(out.dtype)


def sum_kernel(width, p0, p1, p2, p3, out):
    total = p0[...] + p1[...].astype(F32) + p2[...].astype(F32) + p3[...].astype(F32)
    for row in range(total.shape[0]):
        for k in range(total.shape[1] // width):
            out[k, row] = total[row, k * width : (k + 1) * width].astype(BF16)


def call(kernel, outs, scratch, *args, flops=0):
    moved = sum(a.size * a.dtype.itemsize for a in args)
    return pl.pallas_call(
        kernel,
        out_shape=outs,
        in_specs=[VMEM] * len(args),
        out_specs=jax.tree.map(lambda _: VMEM, outs),
        scratch_shapes=scratch,
        cost_estimate=pl.CostEstimate(flops=flops, bytes_accessed=moved, transcendentals=0),
        compiler_params=pltpu.CompilerParams(vmem_limit_bytes=24 * 2**20),
    )(*args)


def over_row(array):
    far = swapped(array, "row", 2)
    return array, swapped(array, "row", 1), far, swapped(far, "row", 1)


def neighbours(first, last):
    size = lax.axis_size("row")
    up = [(i, i + 1) for i in range(size - 1)]
    down = [(j, i) for i, j in up]
    return lax.ppermute(last, "row", up), lax.ppermute(first, "row", down)


def on_device_4x4(frames, w_in, w_out, decay_codes, resets):
    count, height, width, channels = frames.shape
    blocks = count * width
    total = 4 * count
    lanes = channels // 4
    outs = w_out.shape[3]
    marks = jnp.pad(resets.astype(BF16), (0, 8 - count))
    payload = jnp.concatenate(
        [
            frames.transpose(1, 0, 2, 3).reshape(height * blocks, channels),
            jnp.broadcast_to(marks[:, None], (8, channels)),
        ]
    )
    f2 = swapped(payload, "tm", 2)
    f1 = swapped(payload, "tm", 1)
    f3 = swapped(f2, "tm", 1)
    held = (payload, f1, f2, f3)
    up, down = neighbours(
        jnp.stack([f[:blocks] for f in held]),
        jnp.stack([f[(height - 1) * blocks : height * blocks] for f in held]),
    )
    w_blocks = over_row(w_in.transpose(0, 1, 3, 2))
    slab = total * width
    hidden = call(
        functools.partial(drive_kernel, (count, height, width, total)),
        jax.ShapeDtypeStruct((height, slab, lanes), BF16),
        [
            pltpu.VMEM((height + 2, slab, channels), BF16),
            pltpu.VMEM((3, 3, 4, w_in.shape[3], channels), BF16),
            pltpu.VMEM((max(8, total), lanes), F32),
            pltpu.VMEM((height * slab, lanes), F32),
        ],
        *held,
        up,
        down,
        *w_blocks,
        decay_codes.reshape(4, lanes),
        flops=2 * height * slab * 9 * channels * lanes,
    )
    pieces = w_out.transpose(0, 1, 3, 2).reshape(3, 3, outs, 4, lanes)
    z = lax.axis_index("tm")
    mine = [lax.dynamic_index_in_dim(pieces, z ^ d, 3, False) for d in range(4)]
    column = jnp.stack([mine[0]] + [swapped(mine[d], "tm", d) for d in range(1, 4)])
    o_blocks = over_row(column)
    h_up, h_down = neighbours(hidden[:1], hidden[height - 1 :])
    part = functools.partial(jax.ShapeDtypeStruct, (height, blocks, channels))
    parts = call(
        functools.partial(mix_kernel, (count, height, width)),
        (part(F32), part(BF16), part(BF16), part(BF16)),
        [
            pltpu.VMEM((height, slab, 9 * lanes), BF16),
            pltpu.VMEM((channels, 9 * lanes), BF16),
            pltpu.VMEM((height, slab, channels), F32),
        ],
        hidden,
        h_up,
        h_down,
        *o_blocks,
        flops=2 * height * slab * 9 * channels * lanes,
    )
    received = [swapped(parts[d], "tm", d) for d in range(1, 4)]
    return call(
        functools.partial(sum_kernel, width),
        jax.ShapeDtypeStruct(frames.shape, BF16),
        [],
        parts[0],
        *received,
    )


def solution(mesh):
    small = mesh.shape["tm"] == 4 and mesh.shape["row"] == 4
    return jax.shard_map(
        on_device_4x4 if small else on_device,
        mesh=mesh,
        in_specs=(
            P(("grp", "tm"), "row", None, None),
            P(None, None, None, ("tm", "row")),
            P(None, None, None, ("tm", "row")),
            P(),
            P(("grp", "tm")),
        ),
        out_specs=P(("grp", "tm"), "row", None, None),
        check_vma=False,
    )
```

```python
import functools
import math

import jax
import jax.numpy as jnp
from jax import lax
from jax.experimental import pallas as pl
from jax.experimental.pallas import tpu as pltpu
from jax.sharding import PartitionSpec as P


LEVELS = 16
WINDOW = 4096


LOW_LOG = math.log(0.995)
HIGH_LOG = math.log(0.9999)


def entering(part, axis, combine, identity):
    place = lax.axis_index(axis)
    gathered = jax.tree.map(lambda a: lax.all_gather(a, axis), part)
    state = jax.tree.map(lambda a, e: jnp.zeros_like(a) + jnp.asarray(e, a.dtype), part, identity)

    def one(turn, state):
        return combine(
            state, jax.tree.map(lambda a: lax.dynamic_index_in_dim(a, turn, 0, False), gathered)
        )

    return lax.fori_loop(0, place, one, state)


def extended_2(array, sides, width):
    for axis, dim in sides:
        size, length = (lax.axis_size(axis), array.shape[dim])
        up = [(i, (i + 1) % size) for i in range(size - 1)]
        down = [(j, i) for i, j in up]
        last = lax.slice_in_dim(array, length - width, length, axis=dim)
        initial = lax.slice_in_dim(array, 0, width, axis=dim)
        before = lax.ppermute(last, axis, up)
        after = lax.ppermute(initial, axis, down)
        array = jnp.concatenate([before, array, after], axis=dim)
    return array


def frame_rates(decay_codes, frame_count):
    levels = jnp.arange(LEVELS, dtype=jnp.int32)
    log_table = LOW_LOG + levels.astype(jnp.float32) / (LEVELS - 1) * (HIGH_LOG - LOW_LOG)
    picked = (decay_codes[:, None] == levels[None, :]).astype(jnp.float32)
    log_rate = jnp.sum(picked * log_table[None, :], axis=1)
    return jnp.exp(WINDOW / frame_count * log_rate)


def conv_rows(rows, weight):
    count, height, width = (rows.shape[0], rows.shape[1] - 2, rows.shape[2])
    padded = jnp.pad(rows, ((0, 0), (0, 0), (1, 1), (0, 0)))
    total = jnp.zeros((count, height, width, weight.shape[3]), jnp.float32)
    for i in range(3):
        for j in range(3):
            total = total + jnp.einsum(
                "frwc,ck->frwk",
                padded[:, i : i + height, j : j + width],
                weight[i, j],
                preferred_element_type=jnp.float32,
            )
    return total


def carry_combine(earlier, later):
    return (earlier[0] * later[0], later[0][None, None, :] * earlier[1] + later[1])


def recurrence(drive, gates):

    def advance(carry, inputs):
        state, product = carry
        frame_drive, gate = inputs
        state = gate[None, None, :] * state + frame_drive
        product = product * gate
        return ((state, product), (state, product))

    start = (jnp.zeros(drive.shape[1:], jnp.float32), jnp.ones((drive.shape[3],), jnp.float32))
    (last_state, last_product), (states, products) = lax.scan(advance, start, (drive, gates))
    identity = (jnp.ones_like(last_product), jnp.zeros_like(last_state))
    _, before_state = entering((last_product, last_state), "tm", carry_combine, identity)
    return states + products[:, None, None, :] * before_state[None]


def on_device(frames, w_in, w_out, decay_codes, resets):
    frame_count = frames.shape[0] * lax.axis_size("tm")
    rates = frame_rates(decay_codes, frame_count)
    gates = (1.0 - resets.astype(jnp.float32))[:, None] * rates[None, :]
    extended = extended_2(frames, (("row", 1),), 1)
    state = recurrence(
        conv_rows(extended, lax.all_gather(w_in, ("tm", "row"), axis=3, tiled=True)), gates
    )
    hidden = jax.nn.gelu(state).astype(jnp.bfloat16)
    hidden_rows = extended_2(hidden, (("row", 1),), 1)
    return conv_rows(hidden_rows, lax.all_gather(w_out, ("tm", "row"), axis=3, tiled=True)).astype(
        jnp.bfloat16
    )


BF16 = jnp.bfloat16
F32 = jnp.float32
VMEM = pl.BlockSpec(memory_space=pltpu.VMEM)
ANY = pl.BlockSpec(memory_space=pl.ANY)
MARKS = 8


def swapped(array, axis, distance):
    size = lax.axis_size(axis)
    return lax.ppermute(array, axis, [(i, i ^ distance) for i in range(size)])


def across(array):
    pairs = [(i, i + 1) for i in range(1, lax.axis_size("row") - 1, 2)]
    return lax.ppermute(array, "row", pairs + [(j, i) for i, j in pairs])


def dot_nt(a, b):
    return lax.dot_general(a, b, (((1,), (1,)), ((), ())), preferred_element_type=F32)


def shifted_columns(flat, offset, width):
    if offset == 0:
        return flat
    length = flat.shape[0]
    column = lax.rem(lax.broadcasted_iota(jnp.int32, flat.shape, 0), width)
    edge = 0 if offset < 0 else width - 1
    return jnp.where(column == edge, 0.0, pltpu.roll(flat, (-offset) % length, 0))


def payload_kernel(frames_hbm, resets_hbm, out, frames, resets, sem):
    copies = [
        pltpu.make_async_copy(frames_hbm, frames, sem.at[0]),
        pltpu.make_async_copy(resets_hbm, resets, sem.at[1]),
    ]
    for copy in copies:
        copy.start()
    for copy in copies:
        copy.wait()
    count, height, width, channels = frames.shape
    blocks = count * width
    for row in range(height):
        values = jnp.concatenate([frames[k, row].astype(F32) for k in range(count)])
        out[row * blocks : (row + 1) * blocks, :] = values.astype(BF16)
    place = lax.broadcasted_iota(jnp.int32, (MARKS, channels), 0)
    marks = jnp.zeros((MARKS, channels), F32)
    for k in range(count):
        marks = jnp.where(place == k, resets[k].astype(F32), marks)
    out[height * blocks :, :] = marks.astype(BF16)


def pieces_kernel(w, q0, q1, q2, q3):
    z = lax.axis_index("tm")
    lanes = q0.shape[3]
    for d, q in enumerate((q0, q1, q2, q3)):
        here = pl.ds(pl.multiple_of((z ^ d) * lanes, lanes), lanes)
        for i in range(3):
            for j in range(3):
                q[i, j] = w[i, j, :, here]


def drive_kernel(
    dims, f0, f1, f2, f3, e012, e3, near, w0, w1, w2, w3, codes, hid, x, w, gates, states
):
    count, height, width, frame_total = dims
    blocks = count * width
    z, r = lax.axis_index("tm"), lax.axis_index("row")
    odd = lax.rem(r, 2)
    rate = WINDOW / frame_total
    code = codes[pl.ds(z, 1), :].astype(F32)
    rates = jnp.exp(rate * (LOW_LOG + code / (LEVELS - 1) * (HIGH_LOG - LOW_LOG)))
    lanes = rates.shape[1]
    far = (e012.at[0], e012.at[1], e012.at[2], e3)
    for d, f in enumerate((f0, f1, f2, f3)):
        at = z ^ d
        here = pl.ds(pl.multiple_of(at * blocks, blocks), blocks)
        for row in range(height):
            part = slice(row * blocks, (row + 1) * blocks)
            x[height + row, here, :] = f[part, :]
            x[2 * height * odd + row, here, :] = far[d][part, :]
            x[2 * height * (1 - odd) + row, here, :] = near[d, part, :]
        marks = f[height * blocks :, :lanes].astype(F32)
        for k in range(count):
            gates[pl.ds(at * count + k, 1), :] = (1.0 - marks[k : k + 1, :]) * rates
    for d, block in enumerate((w0, w1, w2, w3)):
        for i in range(3):
            for j in range(3):
                w[i, j, pl.ds(r ^ d, 1)] = block[i, j][None]
    slab = x.shape[1]
    shown = height + 2
    total = None
    for i in range(3):
        rows = x[height - 2 + i : height - 2 + i + shown].reshape(shown * slab, x.shape[2])
        term = dot_nt(rows, w[i].reshape(3 * lanes, x.shape[2]))
        total = term if total is None else total + term
    drive = total[:, lanes : 2 * lanes]
    drive = drive + shifted_columns(total[:, :lanes], -1, width)
    drive = drive + shifted_columns(total[:, 2 * lanes :], 1, width)
    for row in range(shown):
        state = jnp.zeros((width, lanes), F32)
        for t in range(frame_total):
            first = row * slab + t * width
            state = gates[t : t + 1, :] * state + drive[first : first + width]
            states[first : first + width, :] = state
    last = lax.axis_size("row") - 1
    for row in range(shown):
        values = jax.nn.gelu(states[row * slab : (row + 1) * slab, :])
        if row == 0:
            values = jnp.where(r == 0, 0.0, values)
        if row == shown - 1:
            values = jnp.where(r == last, 0.0, values)
        hid[row] = values.astype(BF16)


def mix_kernel(dims, hid, q0, g1, g2, g3, x0, x123, c0, cx0, cx123, p0, p1, p2, p3, a, w, part):
    count, height, width = dims
    z, r = lax.axis_index("tm"), lax.axis_index("row")
    outs, lanes = q0.shape[2], q0.shape[3]
    held = (
        (q0, g1, g2, g3),
        tuple(c0.at[e] for e in range(4)),
        (x0,) + tuple(x123.at[e] for e in range(3)),
        (cx0,) + tuple(cx123.at[e] for e in range(3)),
    )
    for d in range(4):
        for e in range(4):
            slot = (z ^ e) * 4 + (r ^ d)
            here = pl.ds(pl.multiple_of(slot * outs, outs), outs)
            for i in range(3):
                for j in range(3):
                    tap = 3 * i + j
                    w[here, tap * lanes : (tap + 1) * lanes] = held[d][e][i, j]
    for row in range(height + 2):
        values = hid[row].astype(F32)
        for j in range(3):
            moved = shifted_columns(values, j - 1, width).astype(BF16)
            for i in range(3):
                out_row = row - i
                if 0 <= out_row < height:
                    tap = 3 * i + j
                    a[out_row, :, tap * lanes : (tap + 1) * lanes] = moved
    for row in range(height):
        part[row] = dot_nt(a[row], w[...])
    blocks = count * width
    for d, out in enumerate((p0, p1, p2, p3)):
        here = pl.ds(pl.multiple_of((z ^ d) * blocks, blocks), blocks)
        for row in range(height):
            out[row] = part[row, here, :].astype(out.dtype)


def sum_kernel(width, p0, p1, p2, p3, out):
    total = p0[...] + p1[...].astype(F32) + p2[...].astype(F32) + p3[...].astype(F32)
    for row in range(total.shape[0]):
        for k in range(total.shape[1] // width):
            out[k, row] = total[row, k * width : (k + 1) * width].astype(BF16)


def call(kernel, outs, scratch, *args, flops=0, specs=None):
    moved = sum(a.size * a.dtype.itemsize for a in args)
    return pl.pallas_call(
        kernel,
        out_shape=outs,
        in_specs=specs or [VMEM] * len(args),
        out_specs=jax.tree.map(lambda _: VMEM, outs),
        scratch_shapes=scratch,
        cost_estimate=pl.CostEstimate(flops=flops, bytes_accessed=moved, transcendentals=0),
        compiler_params=pltpu.CompilerParams(vmem_limit_bytes=24 * 2**20),
    )(*args)


def on_device_4x4(frames, w_in, w_out, decay_codes, resets):
    return staged(frames, w_in, w_out, decay_codes, resets)


def staged(frames, w_in, w_out, decay_codes, resets):
    count, height, width, channels = frames.shape
    blocks = count * width
    total = 4 * count
    lanes = channels // 4
    outs = w_out.shape[3]
    shape = jax.ShapeDtypeStruct
    w0 = w_in.transpose(0, 1, 3, 2)
    w2 = swapped(w0, "row", 2)
    w1 = swapped(w0, "row", 1)
    f0 = call(
        payload_kernel,
        shape((height * blocks + MARKS, channels), BF16),
        [
            pltpu.VMEM(frames.shape, BF16),
            pltpu.SMEM(resets.shape, resets.dtype),
            pltpu.SemaphoreType.DMA((2,)),
        ],
        frames,
        resets,
        specs=[ANY, ANY],
    )
    f2 = swapped(f0, "tm", 2)
    f1 = swapped(f0, "tm", 1)
    piece = shape((3, 3, outs, lanes), BF16)
    q0, q1, q2, q3 = call(pieces_kernel, (piece,) * 4, [], w_out.transpose(0, 1, 3, 2))
    x0 = swapped(q0, "row", 2)
    g2 = swapped(q2, "tm", 2)
    g3 = swapped(q3, "tm", 3)
    f3 = swapped(f2, "tm", 1)
    e012 = across(jnp.stack([f0, f1, f2]))
    g1 = swapped(q1, "tm", 1)
    w3 = swapped(w2, "row", 1)
    e3 = across(f3)
    near = swapped(jnp.stack([f0, f1, f2, f3]), "row", 1)
    x123 = swapped(jnp.stack([g1, g2, g3]), "row", 2)
    c0 = swapped(jnp.stack([q0, g1, g2, g3]), "row", 1)
    cx0 = swapped(x0, "row", 1)
    slab = total * width
    hidden = call(
        functools.partial(drive_kernel, (count, height, width, total)),
        shape((height + 2, slab, lanes), BF16),
        [
            pltpu.VMEM((3 * height, slab, channels), BF16),
            pltpu.VMEM((3, 3, 4, w_in.shape[3], channels), BF16),
            pltpu.VMEM((max(8, total), lanes), F32),
            pltpu.VMEM(((height + 2) * slab, lanes), F32),
        ],
        f0,
        f1,
        f2,
        f3,
        e012,
        e3,
        near,
        w0,
        w1,
        w2,
        w3,
        decay_codes.reshape(4, lanes),
        flops=2 * (height + 2) * slab * 9 * channels * lanes,
    )
    cx123 = swapped(x123, "row", 1)
    part = functools.partial(shape, (height, blocks, channels))
    parts = call(
        functools.partial(mix_kernel, (count, height, width)),
        (part(F32), part(BF16), part(BF16), part(BF16)),
        [
            pltpu.VMEM((height, slab, 9 * lanes), BF16),
            pltpu.VMEM((channels, 9 * lanes), BF16),
            pltpu.VMEM((height, slab, channels), F32),
        ],
        hidden,
        q0,
        g1,
        g2,
        g3,
        x0,
        x123,
        c0,
        cx0,
        cx123,
        flops=2 * height * slab * 9 * channels * lanes,
    )
    received = {d: swapped(parts[d], "tm", d) for d in (3, 2, 1)}
    return call(
        functools.partial(sum_kernel, width),
        shape(frames.shape, BF16),
        [],
        parts[0],
        received[1],
        received[2],
        received[3],
    )


def solution(mesh):
    small = mesh.shape["tm"] == 4 and mesh.shape["row"] == 4
    return jax.shard_map(
        on_device_4x4 if small else on_device,
        mesh=mesh,
        in_specs=(
            P(("grp", "tm"), "row", None, None),
            P(None, None, None, ("tm", "row")),
            P(None, None, None, ("tm", "row")),
            P(),
            P(("grp", "tm")),
        ),
        out_specs=P(("grp", "tm"), "row", None, None),
        check_vma=False,
    )
```

```python
import functools
import math

import jax
import jax.numpy as jnp
from jax import lax
from jax.experimental import pallas as pl
from jax.experimental.pallas import tpu as pltpu
from jax.sharding import PartitionSpec as P


LEVELS = 16
WINDOW = 4096


LOW_LOG = math.log(0.995)
HIGH_LOG = math.log(0.9999)


def entering(part, axis, combine, identity):
    place = lax.axis_index(axis)
    gathered = jax.tree.map(lambda a: lax.all_gather(a, axis), part)
    state = jax.tree.map(lambda a, e: jnp.zeros_like(a) + jnp.asarray(e, a.dtype), part, identity)

    def one(turn, state):
        return combine(
            state, jax.tree.map(lambda a: lax.dynamic_index_in_dim(a, turn, 0, False), gathered)
        )

    return lax.fori_loop(0, place, one, state)


def extended_2(array, sides, width):
    for axis, dim in sides:
        size, length = (lax.axis_size(axis), array.shape[dim])
        up = [(i, (i + 1) % size) for i in range(size - 1)]
        down = [(j, i) for i, j in up]
        last = lax.slice_in_dim(array, length - width, length, axis=dim)
        initial = lax.slice_in_dim(array, 0, width, axis=dim)
        before = lax.ppermute(last, axis, up)
        after = lax.ppermute(initial, axis, down)
        array = jnp.concatenate([before, array, after], axis=dim)
    return array


def frame_rates(decay_codes, frame_count):
    levels = jnp.arange(LEVELS, dtype=jnp.int32)
    log_table = LOW_LOG + levels.astype(jnp.float32) / (LEVELS - 1) * (HIGH_LOG - LOW_LOG)
    picked = (decay_codes[:, None] == levels[None, :]).astype(jnp.float32)
    log_rate = jnp.sum(picked * log_table[None, :], axis=1)
    return jnp.exp(WINDOW / frame_count * log_rate)


def conv_rows(rows, weight):
    count, height, width = (rows.shape[0], rows.shape[1] - 2, rows.shape[2])
    padded = jnp.pad(rows, ((0, 0), (0, 0), (1, 1), (0, 0)))
    total = jnp.zeros((count, height, width, weight.shape[3]), jnp.float32)
    for i in range(3):
        for j in range(3):
            total = total + jnp.einsum(
                "frwc,ck->frwk",
                padded[:, i : i + height, j : j + width],
                weight[i, j],
                preferred_element_type=jnp.float32,
            )
    return total


def carry_combine(earlier, later):
    return (earlier[0] * later[0], later[0][None, None, :] * earlier[1] + later[1])


def recurrence(drive, gates):

    def advance(carry, inputs):
        state, product = carry
        frame_drive, gate = inputs
        state = gate[None, None, :] * state + frame_drive
        product = product * gate
        return ((state, product), (state, product))

    start = (jnp.zeros(drive.shape[1:], jnp.float32), jnp.ones((drive.shape[3],), jnp.float32))
    (last_state, last_product), (states, products) = lax.scan(advance, start, (drive, gates))
    identity = (jnp.ones_like(last_product), jnp.zeros_like(last_state))
    _, before_state = entering((last_product, last_state), "tm", carry_combine, identity)
    return states + products[:, None, None, :] * before_state[None]


def on_device(frames, w_in, w_out, decay_codes, resets):
    frame_count = frames.shape[0] * lax.axis_size("tm")
    rates = frame_rates(decay_codes, frame_count)
    gates = (1.0 - resets.astype(jnp.float32))[:, None] * rates[None, :]
    extended = extended_2(frames, (("row", 1),), 1)
    state = recurrence(
        conv_rows(extended, lax.all_gather(w_in, ("tm", "row"), axis=3, tiled=True)), gates
    )
    hidden = jax.nn.gelu(state).astype(jnp.bfloat16)
    hidden_rows = extended_2(hidden, (("row", 1),), 1)
    return conv_rows(hidden_rows, lax.all_gather(w_out, ("tm", "row"), axis=3, tiled=True)).astype(
        jnp.bfloat16
    )


BF16 = jnp.bfloat16
F32 = jnp.float32
VMEM = pl.BlockSpec(memory_space=pltpu.VMEM)
MARKS = 16


def swapped(array, axis, distance):
    size = lax.axis_size(axis)
    return lax.ppermute(array, axis, [(i, i ^ distance) for i in range(size)])


def across(array):
    pairs = [(i, i + 1) for i in range(1, lax.axis_size("row") - 1, 2)]
    return lax.ppermute(array, "row", pairs + [(j, i) for i, j in pairs])


def dot_nt(a, b):
    return lax.dot_general(a, b, (((1,), (1,)), ((), ())), preferred_element_type=F32)


def shifted_columns(flat, offset, width):
    if offset == 0:
        return flat
    length = flat.shape[0]
    column = lax.rem(lax.broadcasted_iota(jnp.int32, flat.shape, 0), width)
    edge = 0 if offset < 0 else width - 1
    return jnp.where(column == edge, 0.0, pltpu.roll(flat, (-offset) % length, 0))


def pieces_kernel(w, marks, q0, q1, q2, q3):
    z = lax.axis_index("tm")
    outs, lanes = w.shape[2], q0.shape[1]
    for d, q in enumerate((q0, q1, q2, q3)):
        there = pl.ds(pl.multiple_of((z ^ d) * lanes, lanes), lanes)
        for tap in range(9):
            q[tap * outs : (tap + 1) * outs, :] = w[tap // 3, tap % 3, :, there]
        q[9 * outs :, :] = marks[...]


def drive_kernel(
    dims, f0, f1, f2, f3, m0, m1, m2, m3, e012, e3, near, w0, w1, w2, w3, codes, hid, x, w, gates, states
):
    count, height, width, frame_total = dims
    blocks = count * width
    z, r = lax.axis_index("tm"), lax.axis_index("row")
    odd = lax.rem(r, 2)
    rate = WINDOW / frame_total
    code = codes[pl.ds(z, 1), :].astype(F32)
    rates = jnp.exp(rate * (LOW_LOG + code / (LEVELS - 1) * (HIGH_LOG - LOW_LOG)))
    lanes = rates.shape[1]
    far = (e012.at[0], e012.at[1], e012.at[2], e3)
    marks = (m0, m1, m2, m3)
    for d, f in enumerate((f0, f1, f2, f3)):
        at = z ^ d
        here = pl.ds(pl.multiple_of(at * blocks, blocks), blocks)

        def placed(slot, source, row):
            firsts = [(k * height + row) * width for k in range(count)]
            parts = [source[first : first + width, :].astype(F32) for first in firsts]
            x[slot, here, :] = jnp.concatenate(parts).astype(BF16)

        for row in range(height):
            placed(height + row, f, row)
            placed(2 * height * odd + row, far[d], row)
            placed(2 * height * (1 - odd) + row, near.at[d], row)
        mark = marks[d][marks[d].shape[0] - MARKS :, :].astype(F32)
        for k in range(count):
            gates[pl.ds(at * count + k, 1), :] = (1.0 - mark[k : k + 1, :]) * rates
    for d, block in enumerate((w0, w1, w2, w3)):
        for i in range(3):
            for j in range(3):
                w[i, j, pl.ds(r ^ d, 1)] = block[i, j][None]
    slab = x.shape[1]
    shown = height + 2
    total = None
    for i in range(3):
        rows = x[height - 2 + i : height - 2 + i + shown].reshape(shown * slab, x.shape[2])
        term = dot_nt(rows, w[i].reshape(3 * lanes, x.shape[2]))
        total = term if total is None else total + term
    drive = total[:, lanes : 2 * lanes]
    drive = drive + shifted_columns(total[:, :lanes], -1, width)
    drive = drive + shifted_columns(total[:, 2 * lanes :], 1, width)
    for row in range(shown):
        state = jnp.zeros((width, lanes), F32)
        for t in range(frame_total):
            first = row * slab + t * width
            state = gates[t : t + 1, :] * state + drive[first : first + width]
            states[first : first + width, :] = state
    last = lax.axis_size("row") - 1
    for row in range(shown):
        values = jax.nn.gelu(states[row * slab : (row + 1) * slab, :])
        if row == 0:
            values = jnp.where(r == 0, 0.0, values)
        if row == shown - 1:
            values = jnp.where(r == last, 0.0, values)
        hid[row] = values.astype(BF16)


def mix_kernel(dims, hid, *refs):
    count, height, width = dims
    filters, (p0, p1, p2, p3, a, w, part) = refs[:-7], refs[-7:]
    held = []
    for ref in filters:
        held += [ref.at[e] for e in range(ref.shape[0])] if len(ref.shape) == 3 else [ref]
    z, core = lax.axis_index("tm"), lax.rem(lax.axis_index("row"), 2)
    outs, lanes = (held[0].shape[0] - MARKS) // 9, held[0].shape[1]
    for d in range(2):
        for e in range(4):
            slot = (z ^ e) * 2 + (core ^ d)
            here = pl.ds(pl.multiple_of(slot * outs, outs), outs)
            for tap in range(9):
                rows = held[4 * d + e][tap * outs : (tap + 1) * outs, :]
                w[here, tap * lanes : (tap + 1) * lanes] = rows
    for row in range(height + 2):
        values = hid[row].astype(F32)
        for j in range(3):
            moved = shifted_columns(values, j - 1, width).astype(BF16)
            for i in range(3):
                out_row = row - i
                if 0 <= out_row < height:
                    tap = 3 * i + j
                    a[out_row, :, tap * lanes : (tap + 1) * lanes] = moved
    for row in range(height):
        part[row] = dot_nt(a[row], w[...])
    blocks = count * width
    for d, out in enumerate((p0, p1, p2, p3)):
        here = pl.ds(pl.multiple_of((z ^ d) * blocks, blocks), blocks)
        for row in range(height):
            out[row] = part[row, here, :].astype(out.dtype)


def sum_kernel(width, a0, a1, a2, a3, b0, b1, b2, b3, out):
    near = a0[...] + a1[...].astype(F32) + a2[...].astype(F32) + a3[...].astype(F32)
    far = b0[...] + b1[...].astype(F32) + b2[...].astype(F32) + b3[...].astype(F32)
    first = lax.axis_index("row") < 2
    low, high = jnp.where(first, near, far), jnp.where(first, far, near)
    wide = low.shape[2] // 4
    parts = []
    for n in range(4):
        here = slice(n * wide, (n + 1) * wide)
        parts += [low[:, :, here], high[:, :, here]]
    total = jnp.concatenate(parts, axis=2)
    for row in range(total.shape[0]):
        for k in range(total.shape[1] // width):
            out[k, row] = total[row, k * width : (k + 1) * width].astype(BF16)


def call(kernel, outs, scratch, *args, flops=0, specs=None):
    moved = sum(a.size * a.dtype.itemsize for a in args)
    return pl.pallas_call(
        kernel,
        out_shape=outs,
        in_specs=specs or [VMEM] * len(args),
        out_specs=jax.tree.map(lambda _: VMEM, outs),
        scratch_shapes=scratch,
        cost_estimate=pl.CostEstimate(flops=flops, bytes_accessed=moved, transcendentals=0),
        compiler_params=pltpu.CompilerParams(vmem_limit_bytes=24 * 2**20),
    )(*args)


def on_device_4x4(frames, w_in, w_out, decay_codes, resets):
    return staged(frames, w_in, w_out, decay_codes, resets)


def staged(frames, w_in, w_out, decay_codes, resets):
    count, height, width, channels = frames.shape
    blocks = count * width
    total = 4 * count
    lanes = channels // 4
    outs = w_out.shape[3]
    shape = jax.ShapeDtypeStruct
    f0 = frames.reshape(count * height * width, channels)
    f2 = swapped(f0, "tm", 2)
    f1 = swapped(f0, "tm", 1)
    w0 = w_in.transpose(0, 1, 3, 2)
    w2 = swapped(w0, "row", 2)
    w1 = swapped(w0, "row", 1)
    f3 = swapped(f2, "tm", 1)
    e012 = across(jnp.stack([f0, f1, f2]))
    e3 = across(f3)
    near = swapped(jnp.stack([f0, f1, f2, f3]), "row", 1)
    marks = jnp.pad(resets.astype(BF16), (0, MARKS - count))
    marks = jnp.broadcast_to(marks[:, None], (MARKS, lanes))
    piece = shape((9 * outs + MARKS, lanes), BF16)
    q0, q1, q2, q3 = call(pieces_kernel, (piece,) * 4, [], w_out.transpose(0, 1, 3, 2), marks)
    x0 = swapped(q0, "row", 2)
    g1 = swapped(q1, "tm", 1)
    g2 = swapped(q2, "tm", 2)
    g3 = swapped(q3, "tm", 3)
    w3 = swapped(w2, "row", 1)
    x123 = swapped(jnp.stack([g1, g2, g3]), "row", 2)
    c0 = swapped(jnp.stack([q0, g1, g2, g3]), "row", 1)
    cx0 = swapped(x0, "row", 1)
    slab = total * width
    hidden = call(
        functools.partial(drive_kernel, (count, height, width, total)),
        shape((height + 2, slab, lanes), BF16),
        [
            pltpu.VMEM((3 * height, slab, channels), BF16),
            pltpu.VMEM((3, 3, 4, w_in.shape[3], channels), BF16),
            pltpu.VMEM((max(8, total), lanes), F32),
            pltpu.VMEM(((height + 2) * slab, lanes), F32),
        ],
        f0,
        f1,
        f2,
        f3,
        q0,
        g1,
        g2,
        g3,
        e012,
        e3,
        near,
        w0,
        w1,
        w2,
        w3,
        decay_codes.reshape(4, lanes),
        flops=2 * (height + 2) * slab * 9 * channels * lanes,
    )
    cx123 = swapped(x123, "row", 1)
    half = channels // 2
    part = functools.partial(shape, (height, blocks, half))

    def mixed(*filters):
        parts = call(
            functools.partial(mix_kernel, (count, height, width)),
            (part(F32), part(BF16), part(BF16), part(BF16)),
            [
                pltpu.VMEM((height, slab, 9 * lanes), BF16),
                pltpu.VMEM((half, 9 * lanes), BF16),
                pltpu.VMEM((height, slab, half), F32),
            ],
            hidden,
            *filters,
            flops=2 * height * slab * 9 * half * lanes,
        )
        return parts[:1] + tuple(swapped(parts[d], "tm", d) for d in (1, 2, 3))

    own_sums = mixed(q0, g1, g2, g3, c0)
    far_sums = mixed(x0, x123, cx0, cx123)
    return call(
        functools.partial(sum_kernel, width), shape(frames.shape, BF16), [], *own_sums, *far_sums
    )


def solution(mesh):
    small = mesh.shape["tm"] == 4 and mesh.shape["row"] == 4
    return jax.shard_map(
        on_device_4x4 if small else on_device,
        mesh=mesh,
        in_specs=(
            P(("grp", "tm"), "row", None, None),
            P(None, None, None, ("tm", "row")),
            P(None, None, None, ("tm", "row")),
            P(),
            P(("grp", "tm")),
        ),
        out_specs=P(("grp", "tm"), "row", None, None),
        check_vma=False,
    )
```

```python
import functools
import math

import jax
import jax.numpy as jnp
from jax import lax
from jax.experimental import pallas as pl
from jax.experimental.pallas import tpu as pltpu
from jax.sharding import PartitionSpec as P


LEVELS = 16
WINDOW = 4096


LOW_LOG = math.log(0.995)
HIGH_LOG = math.log(0.9999)


def entering(part, axis, combine, identity):
    place = lax.axis_index(axis)
    gathered = jax.tree.map(lambda a: lax.all_gather(a, axis), part)
    state = jax.tree.map(lambda a, e: jnp.zeros_like(a) + jnp.asarray(e, a.dtype), part, identity)

    def one(turn, state):
        return combine(
            state, jax.tree.map(lambda a: lax.dynamic_index_in_dim(a, turn, 0, False), gathered)
        )

    return lax.fori_loop(0, place, one, state)


def extended_2(array, sides, width):
    for axis, dim in sides:
        size, length = (lax.axis_size(axis), array.shape[dim])
        up = [(i, (i + 1) % size) for i in range(size - 1)]
        down = [(j, i) for i, j in up]
        last = lax.slice_in_dim(array, length - width, length, axis=dim)
        initial = lax.slice_in_dim(array, 0, width, axis=dim)
        before = lax.ppermute(last, axis, up)
        after = lax.ppermute(initial, axis, down)
        array = jnp.concatenate([before, array, after], axis=dim)
    return array


def frame_rates(decay_codes, frame_count):
    levels = jnp.arange(LEVELS, dtype=jnp.int32)
    log_table = LOW_LOG + levels.astype(jnp.float32) / (LEVELS - 1) * (HIGH_LOG - LOW_LOG)
    picked = (decay_codes[:, None] == levels[None, :]).astype(jnp.float32)
    log_rate = jnp.sum(picked * log_table[None, :], axis=1)
    return jnp.exp(WINDOW / frame_count * log_rate)


def conv_rows(rows, weight):
    count, height, width = (rows.shape[0], rows.shape[1] - 2, rows.shape[2])
    padded = jnp.pad(rows, ((0, 0), (0, 0), (1, 1), (0, 0)))
    total = jnp.zeros((count, height, width, weight.shape[3]), jnp.float32)
    for i in range(3):
        for j in range(3):
            total = total + jnp.einsum(
                "frwc,ck->frwk",
                padded[:, i : i + height, j : j + width],
                weight[i, j],
                preferred_element_type=jnp.float32,
            )
    return total


def carry_combine(earlier, later):
    return (earlier[0] * later[0], later[0][None, None, :] * earlier[1] + later[1])


def recurrence(drive, gates):

    def advance(carry, inputs):
        state, product = carry
        frame_drive, gate = inputs
        state = gate[None, None, :] * state + frame_drive
        product = product * gate
        return ((state, product), (state, product))

    start = (jnp.zeros(drive.shape[1:], jnp.float32), jnp.ones((drive.shape[3],), jnp.float32))
    (last_state, last_product), (states, products) = lax.scan(advance, start, (drive, gates))
    identity = (jnp.ones_like(last_product), jnp.zeros_like(last_state))
    _, before_state = entering((last_product, last_state), "tm", carry_combine, identity)
    return states + products[:, None, None, :] * before_state[None]


def on_device(frames, w_in, w_out, decay_codes, resets):
    frame_count = frames.shape[0] * lax.axis_size("tm")
    rates = frame_rates(decay_codes, frame_count)
    gates = (1.0 - resets.astype(jnp.float32))[:, None] * rates[None, :]
    extended = extended_2(frames, (("row", 1),), 1)
    state = recurrence(
        conv_rows(extended, lax.all_gather(w_in, ("tm", "row"), axis=3, tiled=True)), gates
    )
    hidden = jax.nn.gelu(state).astype(jnp.bfloat16)
    hidden_rows = extended_2(hidden, (("row", 1),), 1)
    return conv_rows(hidden_rows, lax.all_gather(w_out, ("tm", "row"), axis=3, tiled=True)).astype(
        jnp.bfloat16
    )


BF16 = jnp.bfloat16
F32 = jnp.float32
VMEM = pl.BlockSpec(memory_space=pltpu.VMEM)
MARKS = 16


def swapped(array, axis, distance):
    size = lax.axis_size(axis)
    return lax.ppermute(array, axis, [(i, i ^ distance) for i in range(size)])


def stacked(*arrays):
    return jnp.stack(arrays)


def across(array):
    pairs = [(i, i + 1) for i in range(1, lax.axis_size("row") - 1, 2)]
    return lax.ppermute(array, "row", pairs + [(j, i) for i, j in pairs])


def dot_nt(a, b):
    return lax.dot_general(a, b, (((1,), (1,)), ((), ())), preferred_element_type=F32)


def shifted_columns(flat, offset, width):
    if offset == 0:
        return flat
    length = flat.shape[0]
    column = lax.rem(lax.broadcasted_iota(jnp.int32, flat.shape, 0), width)
    edge = 0 if offset < 0 else width - 1
    return jnp.where(column == edge, 0.0, pltpu.roll(flat, (-offset) % length, 0))


def pieces_kernel(w, marks, q0, q1, q2, q3):
    z = lax.axis_index("tm")
    outs, lanes = w.shape[2], q0.shape[1]
    for d, q in enumerate((q0, q1, q2, q3)):
        there = pl.ds(pl.multiple_of((z ^ d) * lanes, lanes), lanes)
        for tap in range(9):
            q[tap * outs : (tap + 1) * outs, :] = w[tap // 3, tap % 3, :, there]
        q[9 * outs :, :] = marks[...]


def drive_kernel(
    dims, f0, f1, f2, f3, m0, m1, m2, m3, e012, e3, near, w0, w1, w2, w3, codes, hid, x, w, gates, states
):
    count, height, width, frame_total = dims
    blocks = count * width
    z, r = lax.axis_index("tm"), lax.axis_index("row")
    odd = lax.rem(r, 2)
    rate = WINDOW / frame_total
    code = codes[pl.ds(z, 1), :].astype(F32)
    rates = jnp.exp(rate * (LOW_LOG + code / (LEVELS - 1) * (HIGH_LOG - LOW_LOG)))
    lanes = rates.shape[1]
    far = (e012.at[0], e012.at[1], e012.at[2], e3)
    marks = (m0, m1, m2, m3)
    for d, f in enumerate((f0, f1, f2, f3)):
        at = z ^ d
        here = pl.ds(pl.multiple_of(at * blocks, blocks), blocks)

        def placed(slot, source, row):
            firsts = [(k * height + row) * width for k in range(count)]
            parts = [source[first : first + width, :].astype(F32) for first in firsts]
            x[slot, here, :] = jnp.concatenate(parts).astype(BF16)

        for row in range(height):
            placed(height + row, f, row)
            placed(2 * height * odd + row, far[d], row)
            placed(2 * height * (1 - odd) + row, near.at[d], row)
        mark = marks[d][marks[d].shape[0] - MARKS :, :].astype(F32)
        for k in range(count):
            gates[pl.ds(at * count + k, 1), :] = (1.0 - mark[k : k + 1, :]) * rates
    for d, block in enumerate((w0, w1, w2, w3)):
        for i in range(3):
            for j in range(3):
                w[i, j, pl.ds(r ^ d, 1)] = block[i, j][None]
    slab = x.shape[1]
    shown = height + 2
    total = None
    for i in range(3):
        rows = x[height - 2 + i : height - 2 + i + shown].reshape(shown * slab, x.shape[2])
        term = dot_nt(rows, w[i].reshape(3 * lanes, x.shape[2]))
        total = term if total is None else total + term
    drive = total[:, lanes : 2 * lanes]
    drive = drive + shifted_columns(total[:, :lanes], -1, width)
    drive = drive + shifted_columns(total[:, 2 * lanes :], 1, width)
    for row in range(shown):
        state = jnp.zeros((width, lanes), F32)
        for t in range(frame_total):
            first = row * slab + t * width
            state = gates[t : t + 1, :] * state + drive[first : first + width]
            states[first : first + width, :] = state
    last = lax.axis_size("row") - 1
    for row in range(shown):
        values = jax.nn.gelu(states[row * slab : (row + 1) * slab, :])
        if row == 0:
            values = jnp.where(r == 0, 0.0, values)
        if row == shown - 1:
            values = jnp.where(r == last, 0.0, values)
        hid[row] = values.astype(BF16)


def mix_kernel(dims, hid, *refs):
    count, height, width = dims
    filters, (p0, p1, p2, p3, a, w, part) = refs[:-7], refs[-7:]
    held = []
    for ref in filters:
        held += [ref.at[e] for e in range(ref.shape[0])] if len(ref.shape) == 3 else [ref]
    z, core = lax.axis_index("tm"), lax.rem(lax.axis_index("row"), 2)
    outs, lanes = (held[0].shape[0] - MARKS) // 9, held[0].shape[1]
    for d in range(2):
        for e in range(4):
            slot = (z ^ e) * 2 + (core ^ d)
            here = pl.ds(pl.multiple_of(slot * outs, outs), outs)
            for tap in range(9):
                rows = held[4 * d + e][tap * outs : (tap + 1) * outs, :]
                w[here, tap * lanes : (tap + 1) * lanes] = rows
    for row in range(height + 2):
        values = hid[row].astype(F32)
        for j in range(3):
            moved = shifted_columns(values, j - 1, width).astype(BF16)
            for i in range(3):
                out_row = row - i
                if 0 <= out_row < height:
                    tap = 3 * i + j
                    a[out_row, :, tap * lanes : (tap + 1) * lanes] = moved
    for row in range(height):
        part[row] = dot_nt(a[row], w[...])
    blocks = count * width
    for d, out in enumerate((p0, p1, p2, p3)):
        here = pl.ds(pl.multiple_of((z ^ d) * blocks, blocks), blocks)
        for row in range(height):
            out[row] = part[row, here, :].astype(out.dtype)


def sum_kernel(width, a0, a1, a2, a3, b0, b1, b2, b3, out):
    near = a0[...] + a1[...].astype(F32) + a2[...].astype(F32) + a3[...].astype(F32)
    far = b0[...] + b1[...].astype(F32) + b2[...].astype(F32) + b3[...].astype(F32)
    first = lax.axis_index("row") < 2
    low, high = jnp.where(first, near, far), jnp.where(first, far, near)
    wide = low.shape[2] // 4
    parts = []
    for n in range(4):
        here = slice(n * wide, (n + 1) * wide)
        parts += [low[:, :, here], high[:, :, here]]
    total = jnp.concatenate(parts, axis=2)
    for row in range(total.shape[0]):
        for k in range(total.shape[1] // width):
            out[k, row] = total[row, k * width : (k + 1) * width].astype(BF16)


def call(kernel, outs, scratch, *args, flops=0, specs=None):
    moved = sum(a.size * a.dtype.itemsize for a in args)
    return pl.pallas_call(
        kernel,
        out_shape=outs,
        in_specs=specs or [VMEM] * len(args),
        out_specs=jax.tree.map(lambda _: VMEM, outs),
        scratch_shapes=scratch,
        cost_estimate=pl.CostEstimate(flops=flops, bytes_accessed=moved, transcendentals=0),
        compiler_params=pltpu.CompilerParams(vmem_limit_bytes=24 * 2**20),
    )(*args)


def on_device_4x4(frames, w_in, w_out, decay_codes, resets):
    return staged(frames, w_in, w_out, decay_codes, resets)


def staged(frames, w_in, w_out, decay_codes, resets):
    count, height, width, channels = frames.shape
    blocks = count * width
    total = 4 * count
    lanes = channels // 4
    outs = w_out.shape[3]
    shape = jax.ShapeDtypeStruct
    f0 = frames.reshape(count * height * width, channels)
    f2 = swapped(f0, "tm", 2)
    f1 = swapped(f0, "tm", 1)
    w0 = w_in.transpose(0, 1, 3, 2)
    w2 = swapped(w0, "row", 2)
    w1 = swapped(w0, "row", 1)
    f3 = swapped(f2, "tm", 1)
    e012 = across(stacked(f0, f1, f2))
    e3 = across(f3)
    near = swapped(stacked(f0, f1, f2, f3), "row", 1)
    marks = jnp.pad(resets.astype(BF16), (0, MARKS - count))
    marks = jnp.broadcast_to(marks[:, None], (MARKS, lanes))
    piece = shape((9 * outs + MARKS, lanes), BF16)
    q0, q1, q2, q3 = call(pieces_kernel, (piece,) * 4, [], w_out.transpose(0, 1, 3, 2), marks)
    x0 = swapped(q0, "row", 2)
    g1 = swapped(q1, "tm", 1)
    g2 = swapped(q2, "tm", 2)
    g3 = swapped(q3, "tm", 3)
    w3 = swapped(w2, "row", 1)
    x123 = swapped(stacked(g1, g2, g3), "row", 2)
    c0 = swapped(stacked(q0, g1, g2, g3), "row", 1)
    cx0 = swapped(x0, "row", 1)
    slab = total * width
    hidden = call(
        functools.partial(drive_kernel, (count, height, width, total)),
        shape((height + 2, slab, lanes), BF16),
        [
            pltpu.VMEM((3 * height, slab, channels), BF16),
            pltpu.VMEM((3, 3, 4, w_in.shape[3], channels), BF16),
            pltpu.VMEM((max(8, total), lanes), F32),
            pltpu.VMEM(((height + 2) * slab, lanes), F32),
        ],
        f0,
        f1,
        f2,
        f3,
        q0,
        g1,
        g2,
        g3,
        e012,
        e3,
        near,
        w0,
        w1,
        w2,
        w3,
        decay_codes.reshape(4, lanes),
        flops=2 * (height + 2) * slab * 9 * channels * lanes,
    )
    cx123 = swapped(x123, "row", 1)
    half = channels // 2
    part = functools.partial(shape, (height, blocks, half))

    def mixed(*filters):
        parts = call(
            functools.partial(mix_kernel, (count, height, width)),
            (part(F32), part(BF16), part(BF16), part(BF16)),
            [
                pltpu.VMEM((height, slab, 9 * lanes), BF16),
                pltpu.VMEM((half, 9 * lanes), BF16),
                pltpu.VMEM((height, slab, half), F32),
            ],
            hidden,
            *filters,
            flops=2 * height * slab * 9 * half * lanes,
        )
        return parts[:1] + tuple(swapped(parts[d], "tm", d) for d in (1, 2, 3))

    own_sums = mixed(q0, g1, g2, g3, c0)
    far_sums = mixed(x0, x123, cx0, cx123)
    return call(
        functools.partial(sum_kernel, width), shape(frames.shape, BF16), [], *own_sums, *far_sums
    )


def solution(mesh):
    small = mesh.shape["tm"] == 4 and mesh.shape["row"] == 4
    return jax.shard_map(
        on_device_4x4 if small else on_device,
        mesh=mesh,
        in_specs=(
            P(("grp", "tm"), "row", None, None),
            P(None, None, None, ("tm", "row")),
            P(None, None, None, ("tm", "row")),
            P(),
            P(("grp", "tm")),
        ),
        out_specs=P(("grp", "tm"), "row", None, None),
        check_vma=False,
    )
```

```python
import functools
import math

import jax
import jax.numpy as jnp
from jax import lax
from jax.experimental import pallas as pl
from jax.experimental.pallas import tpu as pltpu
from jax.sharding import PartitionSpec as P


LEVELS = 16
WINDOW = 4096


LOW_LOG = math.log(0.995)
HIGH_LOG = math.log(0.9999)


def entering(part, axis, combine, identity):
    place = lax.axis_index(axis)
    gathered = jax.tree.map(lambda a: lax.all_gather(a, axis), part)
    state = jax.tree.map(lambda a, e: jnp.zeros_like(a) + jnp.asarray(e, a.dtype), part, identity)

    def one(turn, state):
        return combine(
            state, jax.tree.map(lambda a: lax.dynamic_index_in_dim(a, turn, 0, False), gathered)
        )

    return lax.fori_loop(0, place, one, state)


def extended_2(array, sides, width):
    for axis, dim in sides:
        size, length = (lax.axis_size(axis), array.shape[dim])
        up = [(i, (i + 1) % size) for i in range(size - 1)]
        down = [(j, i) for i, j in up]
        last = lax.slice_in_dim(array, length - width, length, axis=dim)
        initial = lax.slice_in_dim(array, 0, width, axis=dim)
        before = lax.ppermute(last, axis, up)
        after = lax.ppermute(initial, axis, down)
        array = jnp.concatenate([before, array, after], axis=dim)
    return array


def frame_rates(decay_codes, frame_count):
    levels = jnp.arange(LEVELS, dtype=jnp.int32)
    log_table = LOW_LOG + levels.astype(jnp.float32) / (LEVELS - 1) * (HIGH_LOG - LOW_LOG)
    picked = (decay_codes[:, None] == levels[None, :]).astype(jnp.float32)
    log_rate = jnp.sum(picked * log_table[None, :], axis=1)
    return jnp.exp(WINDOW / frame_count * log_rate)


def conv_rows(rows, weight):
    count, height, width = (rows.shape[0], rows.shape[1] - 2, rows.shape[2])
    padded = jnp.pad(rows, ((0, 0), (0, 0), (1, 1), (0, 0)))
    total = jnp.zeros((count, height, width, weight.shape[3]), jnp.float32)
    for i in range(3):
        for j in range(3):
            total = total + jnp.einsum(
                "frwc,ck->frwk",
                padded[:, i : i + height, j : j + width],
                weight[i, j],
                preferred_element_type=jnp.float32,
            )
    return total


def carry_combine(earlier, later):
    return (earlier[0] * later[0], later[0][None, None, :] * earlier[1] + later[1])


def recurrence(drive, gates):

    def advance(carry, inputs):
        state, product = carry
        frame_drive, gate = inputs
        state = gate[None, None, :] * state + frame_drive
        product = product * gate
        return ((state, product), (state, product))

    start = (jnp.zeros(drive.shape[1:], jnp.float32), jnp.ones((drive.shape[3],), jnp.float32))
    (last_state, last_product), (states, products) = lax.scan(advance, start, (drive, gates))
    identity = (jnp.ones_like(last_product), jnp.zeros_like(last_state))
    _, before_state = entering((last_product, last_state), "tm", carry_combine, identity)
    return states + products[:, None, None, :] * before_state[None]


def on_device(frames, w_in, w_out, decay_codes, resets):
    frame_count = frames.shape[0] * lax.axis_size("tm")
    rates = frame_rates(decay_codes, frame_count)
    gates = (1.0 - resets.astype(jnp.float32))[:, None] * rates[None, :]
    extended = extended_2(frames, (("row", 1),), 1)
    state = recurrence(
        conv_rows(extended, lax.all_gather(w_in, ("tm", "row"), axis=3, tiled=True)), gates
    )
    hidden = jax.nn.gelu(state).astype(jnp.bfloat16)
    hidden_rows = extended_2(hidden, (("row", 1),), 1)
    return conv_rows(hidden_rows, lax.all_gather(w_out, ("tm", "row"), axis=3, tiled=True)).astype(
        jnp.bfloat16
    )


BF16 = jnp.bfloat16
F32 = jnp.float32
VMEM = pl.BlockSpec(memory_space=pltpu.VMEM)
MARKS = 16


def swapped(array, axis, distance):
    size = lax.axis_size(axis)
    return lax.ppermute(array, axis, [(i, i ^ distance) for i in range(size)])


def stacked(*arrays):
    return jnp.stack(arrays)


def across(array):
    pairs = [(i, i + 1) for i in range(1, lax.axis_size("row") - 1, 2)]
    return lax.ppermute(array, "row", pairs + [(j, i) for i, j in pairs])


def dot_nt(a, b):
    return lax.dot_general(a, b, (((1,), (1,)), ((), ())), preferred_element_type=F32)


def shifted_columns(flat, offset, width):
    if offset == 0:
        return flat
    length = flat.shape[0]
    column = lax.rem(lax.broadcasted_iota(jnp.int32, flat.shape, 0), width)
    edge = 0 if offset < 0 else width - 1
    return jnp.where(column == edge, 0.0, pltpu.roll(flat, (-offset) % length, 0))


def pieces_kernel(w, marks, q0, q1, q2, q3):
    z = lax.axis_index("tm")
    outs, lanes = w.shape[2], q0.shape[1]
    for d, q in enumerate((q0, q1, q2, q3)):
        there = pl.ds(pl.multiple_of((z ^ d) * lanes, lanes), lanes)
        for tap in range(9):
            q[tap * outs : (tap + 1) * outs, :] = w[tap // 3, tap % 3, :, there]
        q[9 * outs :, :] = marks[...]


def drive_kernel(
    dims, f0, f1, f2, f3, m0, m1, m2, m3, e012, e3, near, w0, w1, w2, w3, codes, hid, x, w, gates, states
):
    count, height, width, frame_total = dims
    blocks = count * width
    z, r = lax.axis_index("tm"), lax.axis_index("row")
    odd = lax.rem(r, 2)
    rate = WINDOW / frame_total
    code = codes[pl.ds(z, 1), :].astype(F32)
    rates = jnp.exp(rate * (LOW_LOG + code / (LEVELS - 1) * (HIGH_LOG - LOW_LOG)))
    lanes = rates.shape[1]
    far = (e012.at[0], e012.at[1], e012.at[2], e3)
    marks = (m0, m1, m2, m3)
    for d, f in enumerate((f0, f1, f2, f3)):
        at = z ^ d
        here = pl.ds(pl.multiple_of(at * blocks, blocks), blocks)

        def placed(slot, source, row):
            firsts = [(k * height + row) * width for k in range(count)]
            parts = [source[first : first + width, :].astype(F32) for first in firsts]
            x[slot, here, :] = jnp.concatenate(parts).astype(BF16)

        for row in range(height):
            placed(height + row, f, row)
            placed(2 * height * odd + row, far[d], row)
            placed(2 * height * (1 - odd) + row, near.at[d], row)
        mark = marks[d][marks[d].shape[0] - MARKS :, :].astype(F32)
        for k in range(count):
            gates[pl.ds(at * count + k, 1), :] = (1.0 - mark[k : k + 1, :]) * rates
    for d, block in enumerate((w0, w1, w2, w3)):
        for i in range(3):
            for j in range(3):
                w[i, j, pl.ds(r ^ d, 1)] = block[i, j][None]
    slab = x.shape[1]
    shown = height + 2
    total = None
    for i in range(3):
        rows = x[height - 2 + i : height - 2 + i + shown].reshape(shown * slab, x.shape[2])
        term = dot_nt(rows, w[i].reshape(3 * lanes, x.shape[2]))
        total = term if total is None else total + term
    drive = total[:, lanes : 2 * lanes]
    drive = drive + shifted_columns(total[:, :lanes], -1, width)
    drive = drive + shifted_columns(total[:, 2 * lanes :], 1, width)
    for row in range(shown):
        state = jnp.zeros((width, lanes), F32)
        for t in range(frame_total):
            first = row * slab + t * width
            state = gates[t : t + 1, :] * state + drive[first : first + width]
            states[first : first + width, :] = state
    last = lax.axis_size("row") - 1
    for row in range(shown):
        values = jax.nn.gelu(states[row * slab : (row + 1) * slab, :])
        if row == 0:
            values = jnp.where(r == 0, 0.0, values)
        if row == shown - 1:
            values = jnp.where(r == last, 0.0, values)
        for j in range(3):
            moved = shifted_columns(values, j - 1, width).astype(BF16)
            for i in range(3):
                if 0 <= row - i < height:
                    tap = 3 * i + j
                    hid[row - i, :, tap * lanes : (tap + 1) * lanes] = moved


def mix_kernel(dims, hid, *refs):
    count, height, width = dims
    filters, (p0, p1, p2, p3, w, part) = refs[:-6], refs[-6:]
    held = []
    for ref in filters:
        held += [ref.at[e] for e in range(ref.shape[0])] if len(ref.shape) == 3 else [ref]
    z, core = lax.axis_index("tm"), lax.rem(lax.axis_index("row"), 2)
    outs, lanes = (held[0].shape[0] - MARKS) // 9, held[0].shape[1]
    for d in range(2):
        for e in range(4):
            slot = (z ^ e) * 2 + (core ^ d)
            here = pl.ds(pl.multiple_of(slot * outs, outs), outs)
            for tap in range(9):
                rows = held[4 * d + e][tap * outs : (tap + 1) * outs, :]
                w[here, tap * lanes : (tap + 1) * lanes] = rows
    slab = hid.shape[1]
    part[...] = dot_nt(hid[...].reshape(height * slab, hid.shape[2]), w[...]).reshape(part.shape)
    blocks = count * width
    for d, out in enumerate((p0, p1, p2, p3)):
        here = pl.ds(pl.multiple_of((z ^ d) * blocks, blocks), blocks)
        for row in range(height):
            out[row] = part[row, here, :].astype(out.dtype)


def sum_kernel(width, a0, a1, a2, a3, b0, b1, b2, b3, out):
    near = a0[...] + a1[...].astype(F32) + a2[...].astype(F32) + a3[...].astype(F32)
    far = b0[...] + b1[...].astype(F32) + b2[...].astype(F32) + b3[...].astype(F32)
    first = lax.axis_index("row") < 2
    low, high = jnp.where(first, near, far), jnp.where(first, far, near)
    wide = low.shape[2] // 4
    parts = []
    for n in range(4):
        here = slice(n * wide, (n + 1) * wide)
        parts += [low[:, :, here], high[:, :, here]]
    total = jnp.concatenate(parts, axis=2)
    for row in range(total.shape[0]):
        for k in range(total.shape[1] // width):
            out[k, row] = total[row, k * width : (k + 1) * width].astype(BF16)


def call(kernel, outs, scratch, *args, flops=0, specs=None):
    moved = sum(a.size * a.dtype.itemsize for a in args)
    return pl.pallas_call(
        kernel,
        out_shape=outs,
        in_specs=specs or [VMEM] * len(args),
        out_specs=jax.tree.map(lambda _: VMEM, outs),
        scratch_shapes=scratch,
        cost_estimate=pl.CostEstimate(flops=flops, bytes_accessed=moved, transcendentals=0),
        compiler_params=pltpu.CompilerParams(vmem_limit_bytes=24 * 2**20),
    )(*args)


def on_device_4x4(frames, w_in, w_out, decay_codes, resets):
    return staged(frames, w_in, w_out, decay_codes, resets)


def staged(frames, w_in, w_out, decay_codes, resets):
    count, height, width, channels = frames.shape
    blocks = count * width
    total = 4 * count
    lanes = channels // 4
    outs = w_out.shape[3]
    shape = jax.ShapeDtypeStruct
    f0 = frames.reshape(count * height * width, channels)
    f2 = swapped(f0, "tm", 2)
    f1 = swapped(f0, "tm", 1)
    w0 = w_in.transpose(0, 1, 3, 2)
    w2 = swapped(w0, "row", 2)
    w1 = swapped(w0, "row", 1)
    f3 = swapped(f2, "tm", 1)
    e012 = across(stacked(f0, f1, f2))
    e3 = across(f3)
    near = swapped(stacked(f0, f1, f2, f3), "row", 1)
    marks = jnp.pad(resets.astype(BF16), (0, MARKS - count))
    marks = jnp.broadcast_to(marks[:, None], (MARKS, lanes))
    piece = shape((9 * outs + MARKS, lanes), BF16)
    q0, q1, q2, q3 = call(pieces_kernel, (piece,) * 4, [], w_out.transpose(0, 1, 3, 2), marks)
    x0 = swapped(q0, "row", 2)
    g1 = swapped(q1, "tm", 1)
    g2 = swapped(q2, "tm", 2)
    g3 = swapped(q3, "tm", 3)
    w3 = swapped(w2, "row", 1)
    x123 = swapped(stacked(g1, g2, g3), "row", 2)
    c0 = swapped(stacked(q0, g1, g2, g3), "row", 1)
    cx0 = swapped(x0, "row", 1)
    slab = total * width
    hidden = call(
        functools.partial(drive_kernel, (count, height, width, total)),
        shape((height, slab, 9 * lanes), BF16),
        [
            pltpu.VMEM((3 * height, slab, channels), BF16),
            pltpu.VMEM((3, 3, 4, w_in.shape[3], channels), BF16),
            pltpu.VMEM((max(8, total), lanes), F32),
            pltpu.VMEM(((height + 2) * slab, lanes), F32),
        ],
        f0,
        f1,
        f2,
        f3,
        q0,
        g1,
        g2,
        g3,
        e012,
        e3,
        near,
        w0,
        w1,
        w2,
        w3,
        decay_codes.reshape(4, lanes),
        flops=2 * (height + 2) * slab * 9 * channels * lanes,
    )
    cx123 = swapped(x123, "row", 1)
    half = channels // 2
    part = functools.partial(shape, (height, blocks, half))

    def mixed(*filters):
        parts = call(
            functools.partial(mix_kernel, (count, height, width)),
            (part(F32), part(BF16), part(BF16), part(BF16)),
            [
                pltpu.VMEM((half, 9 * lanes), BF16),
                pltpu.VMEM((height, slab, half), F32),
            ],
            hidden,
            *filters,
            flops=2 * height * slab * 9 * half * lanes,
        )
        return parts[:1] + tuple(swapped(parts[d], "tm", d) for d in (1, 2, 3))

    own_sums = mixed(q0, g1, g2, g3, c0)
    far_sums = mixed(x0, x123, cx0, cx123)
    return call(
        functools.partial(sum_kernel, width), shape(frames.shape, BF16), [], *own_sums, *far_sums
    )


def solution(mesh):
    small = mesh.shape["tm"] == 4 and mesh.shape["row"] == 4
    return jax.shard_map(
        on_device_4x4 if small else on_device,
        mesh=mesh,
        in_specs=(
            P(("grp", "tm"), "row", None, None),
            P(None, None, None, ("tm", "row")),
            P(None, None, None, ("tm", "row")),
            P(),
            P(("grp", "tm")),
        ),
        out_specs=P(("grp", "tm"), "row", None, None),
        check_vma=False,
    )
```

```python
import functools
import math

import jax
import jax.numpy as jnp
from jax import lax
from jax.experimental import pallas as pl
from jax.experimental.pallas import tpu as pltpu
from jax.sharding import PartitionSpec as P


LEVELS = 16
WINDOW = 4096


LOW_LOG = math.log(0.995)
HIGH_LOG = math.log(0.9999)


def entering(part, axis, combine, identity):
    place = lax.axis_index(axis)
    gathered = jax.tree.map(lambda a: lax.all_gather(a, axis), part)
    state = jax.tree.map(lambda a, e: jnp.zeros_like(a) + jnp.asarray(e, a.dtype), part, identity)

    def one(turn, state):
        return combine(
            state, jax.tree.map(lambda a: lax.dynamic_index_in_dim(a, turn, 0, False), gathered)
        )

    return lax.fori_loop(0, place, one, state)


def extended_2(array, sides, width):
    for axis, dim in sides:
        size, length = (lax.axis_size(axis), array.shape[dim])
        up = [(i, (i + 1) % size) for i in range(size - 1)]
        down = [(j, i) for i, j in up]
        last = lax.slice_in_dim(array, length - width, length, axis=dim)
        initial = lax.slice_in_dim(array, 0, width, axis=dim)
        before = lax.ppermute(last, axis, up)
        after = lax.ppermute(initial, axis, down)
        array = jnp.concatenate([before, array, after], axis=dim)
    return array


def frame_rates(decay_codes, frame_count):
    levels = jnp.arange(LEVELS, dtype=jnp.int32)
    log_table = LOW_LOG + levels.astype(jnp.float32) / (LEVELS - 1) * (HIGH_LOG - LOW_LOG)
    picked = (decay_codes[:, None] == levels[None, :]).astype(jnp.float32)
    log_rate = jnp.sum(picked * log_table[None, :], axis=1)
    return jnp.exp(WINDOW / frame_count * log_rate)


def conv_rows(rows, weight):
    count, height, width = (rows.shape[0], rows.shape[1] - 2, rows.shape[2])
    padded = jnp.pad(rows, ((0, 0), (0, 0), (1, 1), (0, 0)))
    total = jnp.zeros((count, height, width, weight.shape[3]), jnp.float32)
    for i in range(3):
        for j in range(3):
            total = total + jnp.einsum(
                "frwc,ck->frwk",
                padded[:, i : i + height, j : j + width],
                weight[i, j],
                preferred_element_type=jnp.float32,
            )
    return total


def carry_combine(earlier, later):
    return (earlier[0] * later[0], later[0][None, None, :] * earlier[1] + later[1])


def recurrence(drive, gates):

    def advance(carry, inputs):
        state, product = carry
        frame_drive, gate = inputs
        state = gate[None, None, :] * state + frame_drive
        product = product * gate
        return ((state, product), (state, product))

    start = (jnp.zeros(drive.shape[1:], jnp.float32), jnp.ones((drive.shape[3],), jnp.float32))
    (last_state, last_product), (states, products) = lax.scan(advance, start, (drive, gates))
    identity = (jnp.ones_like(last_product), jnp.zeros_like(last_state))
    _, before_state = entering((last_product, last_state), "tm", carry_combine, identity)
    return states + products[:, None, None, :] * before_state[None]


def on_device(frames, w_in, w_out, decay_codes, resets):
    frame_count = frames.shape[0] * lax.axis_size("tm")
    rates = frame_rates(decay_codes, frame_count)
    gates = (1.0 - resets.astype(jnp.float32))[:, None] * rates[None, :]
    extended = extended_2(frames, (("row", 1),), 1)
    state = recurrence(
        conv_rows(extended, lax.all_gather(w_in, ("tm", "row"), axis=3, tiled=True)), gates
    )
    hidden = jax.nn.gelu(state).astype(jnp.bfloat16)
    hidden_rows = extended_2(hidden, (("row", 1),), 1)
    return conv_rows(hidden_rows, lax.all_gather(w_out, ("tm", "row"), axis=3, tiled=True)).astype(
        jnp.bfloat16
    )


BF16 = jnp.bfloat16
F32 = jnp.float32
VMEM = pl.BlockSpec(memory_space=pltpu.VMEM)
MARKS = 16


def swapped(array, axis, distance):
    size = lax.axis_size(axis)
    return lax.ppermute(array, axis, [(i, i ^ distance) for i in range(size)])


def stacked(*arrays):
    return jnp.stack(arrays)


def across(array):
    pairs = [(i, i + 1) for i in range(1, lax.axis_size("row") - 1, 2)]
    return lax.ppermute(array, "row", pairs + [(j, i) for i, j in pairs])


def dot_nt(a, b):
    return lax.dot_general(a, b, (((1,), (1,)), ((), ())), preferred_element_type=F32)


def shifted_columns(flat, offset, width):
    if offset == 0:
        return flat
    length = flat.shape[0]
    column = lax.rem(lax.broadcasted_iota(jnp.int32, flat.shape, 0), width)
    edge = 0 if offset < 0 else width - 1
    return jnp.where(column == edge, 0.0, pltpu.roll(flat, (-offset) % length, 0))


def pieces_kernel(w, marks, q0, q1, q2, q3):
    z = lax.axis_index("tm")
    outs, lanes = w.shape[2], q0.shape[1]
    for d, q in enumerate((q0, q1, q2, q3)):
        there = pl.ds(pl.multiple_of((z ^ d) * lanes, lanes), lanes)
        for tap in range(9):
            q[tap * outs : (tap + 1) * outs, :] = w[tap // 3, tap % 3, :, there]
        q[9 * outs :, :] = marks[...]


def drive_kernel(
    dims, f0, f1, f2, f3, m0, m1, m2, m3, e012, e3, near, w0, w1, w2, w3, codes, hid, x, w, gates, states
):
    count, height, width, frame_total = dims
    blocks = count * width
    z, r = lax.axis_index("tm"), lax.axis_index("row")
    odd = lax.rem(r, 2)
    rate = WINDOW / frame_total
    code = codes[pl.ds(z, 1), :].astype(F32)
    rates = jnp.exp(rate * (LOW_LOG + code / (LEVELS - 1) * (HIGH_LOG - LOW_LOG)))
    lanes = rates.shape[1]
    far = (e012.at[0], e012.at[1], e012.at[2], e3)
    marks = (m0, m1, m2, m3)
    for d, f in enumerate((f0, f1, f2, f3)):
        at = z ^ d
        here = pl.ds(pl.multiple_of(at * blocks, blocks), blocks)

        def placed(slot, source, row):
            firsts = [(k * height + row) * width for k in range(count)]
            parts = [source[first : first + width, :].astype(F32) for first in firsts]
            x[slot, here, :] = jnp.concatenate(parts).astype(BF16)

        for row in range(height):
            placed(height + row, f, row)
            placed(2 * height * odd + row, far[d], row)
            placed(2 * height * (1 - odd) + row, near.at[d], row)
        mark = marks[d][marks[d].shape[0] - MARKS :, :].astype(F32)
        for k in range(count):
            gates[pl.ds(at * count + k, 1), :] = (1.0 - mark[k : k + 1, :]) * rates
    for d, block in enumerate((w0, w1, w2, w3)):
        for i in range(3):
            for j in range(3):
                w[i, j, pl.ds(r ^ d, 1)] = block[i, j][None]
    slab = x.shape[1]
    shown = height + 2
    total = None
    for i in range(3):
        rows = x[height - 2 + i : height - 2 + i + shown].reshape(shown * slab, x.shape[2])
        term = dot_nt(rows, w[i].reshape(3 * lanes, x.shape[2]))
        total = term if total is None else total + term
    drive = total[:, lanes : 2 * lanes]
    drive = drive + shifted_columns(total[:, :lanes], -1, width)
    drive = drive + shifted_columns(total[:, 2 * lanes :], 1, width)
    for row in range(shown):
        state = jnp.zeros((width, lanes), F32)
        for t in range(frame_total):
            first = row * slab + t * width
            state = gates[t : t + 1, :] * state + drive[first : first + width]
            states[first : first + width, :] = state
    last = lax.axis_size("row") - 1
    for row in range(shown):
        values = jax.nn.gelu(states[row * slab : (row + 1) * slab, :])
        if row == 0:
            values = jnp.where(r == 0, 0.0, values)
        if row == shown - 1:
            values = jnp.where(r == last, 0.0, values)
        for j in range(3):
            moved = shifted_columns(values, j - 1, width).astype(BF16)
            for i in range(3):
                if 0 <= row - i < height:
                    tap = 3 * i + j
                    hid[row - i, :, tap * lanes : (tap + 1) * lanes] = moved


def mix_kernel(dims, hid, *refs):
    count, height, width = dims
    filters, (p0, p1, p2, p3, w, part) = refs[:-6], refs[-6:]
    held = []
    for ref in filters:
        held += [ref.at[e] for e in range(ref.shape[0])] if len(ref.shape) == 3 else [ref]
    z, core = lax.axis_index("tm"), lax.rem(lax.axis_index("row"), 2)
    outs, lanes = (held[0].shape[0] - MARKS) // 9, held[0].shape[1]
    for d in range(2):
        for e in range(4):
            slot = (z ^ e) * 2 + (core ^ d)
            here = pl.ds(pl.multiple_of(slot * outs, outs), outs)
            for tap in range(9):
                rows = held[4 * d + e][tap * outs : (tap + 1) * outs, :]
                w[here, tap * lanes : (tap + 1) * lanes] = rows
    slab = hid.shape[1]
    part[...] = dot_nt(hid[...].reshape(height * slab, hid.shape[2]), w[...]).reshape(part.shape)
    blocks = count * width
    for d, out in enumerate((p0, p1, p2, p3)):
        here = pl.ds(pl.multiple_of((z ^ d) * blocks, blocks), blocks)
        for row in range(height):
            out[row] = part[row, here, :].astype(out.dtype)


def near_kernel(a0, a1, a2, a3, near):
    near[...] = a0[...] + a1[...].astype(F32) + a2[...].astype(F32) + a3[...].astype(F32)


def sum_kernel(width, near_ref, b0, b1, b2, b3, out):
    near = near_ref[...]
    far = b0[...] + b1[...].astype(F32) + b2[...].astype(F32) + b3[...].astype(F32)
    first = lax.axis_index("row") < 2
    low, high = jnp.where(first, near, far), jnp.where(first, far, near)
    wide = low.shape[2] // 4
    parts = []
    for n in range(4):
        here = slice(n * wide, (n + 1) * wide)
        parts += [low[:, :, here], high[:, :, here]]
    total = jnp.concatenate(parts, axis=2)
    for row in range(total.shape[0]):
        for k in range(total.shape[1] // width):
            out[k, row] = total[row, k * width : (k + 1) * width].astype(BF16)


def call(kernel, outs, scratch, *args, flops=0, specs=None):
    moved = sum(a.size * a.dtype.itemsize for a in args)
    return pl.pallas_call(
        kernel,
        out_shape=outs,
        in_specs=specs or [VMEM] * len(args),
        out_specs=jax.tree.map(lambda _: VMEM, outs),
        scratch_shapes=scratch,
        cost_estimate=pl.CostEstimate(flops=flops, bytes_accessed=moved, transcendentals=0),
        compiler_params=pltpu.CompilerParams(vmem_limit_bytes=24 * 2**20),
    )(*args)


def on_device_4x4(frames, w_in, w_out, decay_codes, resets):
    return staged(frames, w_in, w_out, decay_codes, resets)


def staged(frames, w_in, w_out, decay_codes, resets):
    count, height, width, channels = frames.shape
    blocks = count * width
    total = 4 * count
    lanes = channels // 4
    outs = w_out.shape[3]
    shape = jax.ShapeDtypeStruct
    f0 = frames.reshape(count * height * width, channels)
    f2 = swapped(f0, "tm", 2)
    f1 = swapped(f0, "tm", 1)
    w0 = w_in.transpose(0, 1, 3, 2)
    w2 = swapped(w0, "row", 2)
    w1 = swapped(w0, "row", 1)
    f3 = swapped(f2, "tm", 1)
    e012 = across(stacked(f0, f1, f2))
    e3 = across(f3)
    near = swapped(stacked(f0, f1, f2, f3), "row", 1)
    marks = jnp.pad(resets.astype(BF16), (0, MARKS - count))
    marks = jnp.broadcast_to(marks[:, None], (MARKS, lanes))
    piece = shape((9 * outs + MARKS, lanes), BF16)
    q0, q1, q2, q3 = call(pieces_kernel, (piece,) * 4, [], w_out.transpose(0, 1, 3, 2), marks)
    x0 = swapped(q0, "row", 2)
    g1 = swapped(q1, "tm", 1)
    g2 = swapped(q2, "tm", 2)
    g3 = swapped(q3, "tm", 3)
    w3 = swapped(w2, "row", 1)
    x123 = swapped(stacked(g1, g2, g3), "row", 2)
    c0 = swapped(stacked(q0, g1, g2, g3), "row", 1)
    cx0 = swapped(x0, "row", 1)
    slab = total * width
    hidden = call(
        functools.partial(drive_kernel, (count, height, width, total)),
        shape((height, slab, 9 * lanes), BF16),
        [
            pltpu.VMEM((3 * height, slab, channels), BF16),
            pltpu.VMEM((3, 3, 4, w_in.shape[3], channels), BF16),
            pltpu.VMEM((max(8, total), lanes), F32),
            pltpu.VMEM(((height + 2) * slab, lanes), F32),
        ],
        f0,
        f1,
        f2,
        f3,
        q0,
        g1,
        g2,
        g3,
        e012,
        e3,
        near,
        w0,
        w1,
        w2,
        w3,
        decay_codes.reshape(4, lanes),
        flops=2 * (height + 2) * slab * 9 * channels * lanes,
    )
    cx123 = swapped(x123, "row", 1)
    half = channels // 2
    part = functools.partial(shape, (height, blocks, half))

    def mixed(*filters):
        parts = call(
            functools.partial(mix_kernel, (count, height, width)),
            (part(F32), part(BF16), part(BF16), part(BF16)),
            [
                pltpu.VMEM((half, 9 * lanes), BF16),
                pltpu.VMEM((height, slab, half), F32),
            ],
            hidden,
            *filters,
            flops=2 * height * slab * 9 * half * lanes,
        )
        return parts[:1] + tuple(swapped(parts[d], "tm", d) for d in (1, 2, 3))

    own_sums = mixed(q0, g1, g2, g3, c0)
    far_sums = mixed(x0, x123, cx0, cx123)
    near = call(near_kernel, shape(own_sums[0].shape, F32), [], *own_sums)
    return call(
        functools.partial(sum_kernel, width), shape(frames.shape, BF16), [], near, *far_sums
    )


def solution(mesh):
    small = mesh.shape["tm"] == 4 and mesh.shape["row"] == 4
    return jax.shard_map(
        on_device_4x4 if small else on_device,
        mesh=mesh,
        in_specs=(
            P(("grp", "tm"), "row", None, None),
            P(None, None, None, ("tm", "row")),
            P(None, None, None, ("tm", "row")),
            P(),
            P(("grp", "tm")),
        ),
        out_specs=P(("grp", "tm"), "row", None, None),
        check_vma=False,
    )
```
